32 devices in a mesh: ga: 2 (over y), gx: 4 (over z), gy: 2 (over x), gz: 2 (over core).
Axes of the slice: x: 2, y: 2, z: 4, core: 2. Of those that a mesh axis runs over, the one named last changes fastest.
Arguments:
- state: bfloat16 [8, 256, 4, 512], P(('ga', 'gx'), None, None, 'gy'), parts along dimension 0, may hold values from -6 to 6
- left_env: bfloat16 [16, 8, 256, 256], P(None, ('ga', 'gx')), parts along dimension 1, may hold values from -0.375 to 0.375
- mpo_terms: bfloat16 [16, 16, 4, 4], P(None, 'gz'), may hold values from -0.75 to 0.75
- right_env: bfloat16 [16, 1024, 256], P('gz', ('ga', 'gy')), parts along dimension 1, may hold values from -0.09375 to 0.09375
- term_charge: int32 [16], replicated, may hold values from 0 to 2, as said below
- charge_order: int32 [8], P('ga'), parts along dimension 0, may hold values from 0 to 3, as said below
- sector_dims: int32 [8], P('ga'), parts along dimension 0, may hold values from 128 to 256
Outputs:
- result_state: bfloat16 [8, 256, 4, 512], P(('ga', 'gx'), None, 'gz', 'gy'), parts along dimension 0
The draws below stay inside these ranges and needn't reach their ends.
There are 2 independent parts, one for each index of `ga`. The reference program is written for one: setup_inputs(seed, part) draws one part's arguments, and reference() takes and returns one part's arrays. A program takes and returns all parts, laid end to end along the dimension named above; an argument that names none is the same for every part. Nothing has to cross between parts.
Inputs may be any that keep to these rules, and one draw needn't show every extreme that they name: `charge_order`: each value appears once. `term_charge`: each of 0, 1 and 2 appears at least once.
All inputs are finite; a program needn't handle non-finite values.
Results may differ from the reference program's by a relative error of at most 0.0057.
Values may be sent and summed in bfloat16 or wider, within the bound.
No kernel may reach another device: no remote copies, remote signals or barrier semaphores. Data moves between devices by JAX's collectives and lax.ppermute only.
A program may use at most 64 MiB of HBM per device.

```python
import jax
import jax.numpy as jnp
from jax import lax

BLK = 256
P_SIZE = 4
RB = 256
W = 16
NS = 4
NR = 512


def draw_charge_order(key, part):
    half_count = NS // 2
    order_key = jax.random.fold_in(key, 11)
    flip_key = jax.random.fold_in(key, 12)
    pair_ids = jax.random.permutation(order_key, half_count).astype(jnp.int32)
    flips = jax.random.randint(flip_key, (half_count,), 0, 2).astype(jnp.int32)
    lower = 2 * pair_ids + flips
    upper = 2 * pair_ids + 1 - flips
    return jnp.concatenate([lower, upper]).astype(jnp.int32)


def draw_term_charge(key, part):
    base_key = jax.random.fold_in(key, 21)
    place_key = jax.random.fold_in(key, 22)
    base = jax.random.randint(base_key, (W,), 0, 3).astype(jnp.int32)
    placing = jax.random.permutation(place_key, W).astype(jnp.int32)
    inverse = jnp.argsort(placing).astype(jnp.int32)
    return jnp.where(inverse < 3, inverse, base).astype(jnp.int32)


def with_ends(result, stream_key, low, top_value):
    longest = result.shape.index(max(result.shape))
    spots = []
    for shift in (0, 1):
        where = [jax.random.randint(jax.random.fold_in(stream_key, axis), (), 0, length) for axis, length in enumerate(result.shape)]
        where[longest] = (where[longest] + shift) % result.shape[longest]
        spots.append(tuple(where))
    return result.at[spots[0]].set(low).at[spots[1]].set(top_value)


def shard_levels(key, extent, split, low, top_value):
    loudness, own = 1.0, jax.random.fold_in(key, 6)
    for dim, shards_of in split:
        draws = jnp.exp(jax.random.uniform(jax.random.fold_in(own, dim), (shards_of,), jnp.float32, low / len(split), top_value / len(split)))
        loudness = loudness * jnp.repeat(draws, extent[dim] // shards_of).reshape([-1 if axis == dim else 1 for axis in range(len(extent))])
    return loudness


def noise(own_key, extent, width, bound, split=(), held_as=jnp.bfloat16):
    array = jax.random.normal(own_key, extent, jnp.float32) * width
    if len(split) > 0:
        array = shard_levels(own_key, extent, split, -0.22, 0.18) * array
    return jnp.clip(array, min=-bound, max=bound).astype(held_as)


def setup_inputs(seed: int = 0, part: int = 0) -> dict:
    seeds = jax.random.split(jax.random.key(seed), 8)
    part_splits = jax.random.split(jax.random.fold_in(seeds[7], part), 8)
    return {
        "state": noise(part_splits[0], (NS, BLK, P_SIZE, NR), 1.0, 6.0, ((0, 4), (3, 2))),
        "left_env": noise(part_splits[1], (W, NS, BLK, BLK), BLK ** -0.5, 0.375, ((1, 4),)),
        "mpo_terms": noise(seeds[2], (W, W, P_SIZE, P_SIZE), (W * P_SIZE) ** -0.5, 0.75, ((1, 2),)),
        "right_env": noise(part_splits[3], (W, NR, RB), (W * RB) ** -0.5, 0.09375, ((0, 2), (1, 2))),
        "term_charge": draw_term_charge(jax.random.fold_in(seeds[7], 71), part),
        "charge_order": draw_charge_order(jax.random.fold_in(jax.random.fold_in(seeds[7], part), 71), part),
        "sector_dims": with_ends(jax.random.randint(part_splits[6], (NS,), BLK // 2, BLK + 1), jax.random.fold_in(part_splits[6], 1), BLK // 2, BLK).astype(jnp.int32),
    }


def source_table(charge_order, first_sector, sector_count):
    own_charge = lax.dynamic_slice_in_dim(charge_order, first_sector, sector_count, 0)
    wanted = own_charge[:, None] + jnp.arange(3, dtype=jnp.int32)[None, :] - 1
    matches = charge_order[None, None, :] == wanted[:, :, None]
    sector_ids = jnp.arange(charge_order.shape[0], dtype=jnp.int32)
    found_ids = jnp.sum(jnp.where(matches, sector_ids[None, None, :], 0), axis=2).astype(jnp.int32)
    return jnp.where(jnp.any(matches, axis=2), found_ids, -1).astype(jnp.int32)


def reference(state, left_env, mpo_terms, right_env, term_charge, charge_order, sector_dims):
    sector_count = charge_order.shape[0]
    sources = source_table(charge_order, 0, sector_count)
    term_count = right_env.shape[0]
    tile_width = right_env.shape[2]
    tile_count = right_env.shape[1] // tile_width
    right_tiles = right_env.astype(jnp.float32).reshape(term_count, tile_count, tile_width, tile_width)
    mpo_float = mpo_terms.astype(jnp.float32)
    row_count = state.shape[1]
    phys = state.shape[2]
    rows_iota = jnp.arange(row_count, dtype=jnp.int32)

    def one_sector(sector):
        sector_src = sources[sector]
        safe_src = jnp.clip(sector_src, 0, sector_count - 1).astype(jnp.int32)
        blocks = state[safe_src].astype(jnp.float32) * (sector_src >= 0).astype(jnp.float32)[:, None, None, None]
        chosen = blocks[term_charge]
        environment = left_env[:, sector].astype(jnp.float32)
        applied = jnp.einsum('wxa,wapb->wxpb', environment, chosen).astype(jnp.bfloat16)
        mixed_terms = jnp.einsum('uvpq,uxqb->vxpb', mpo_float, applied.astype(jnp.float32)).astype(jnp.bfloat16)
        mixed_terms = mixed_terms.astype(jnp.float32).reshape(term_count, row_count, phys, tile_count, tile_width)
        tile_total = jnp.einsum('vxptb,vtbc->xptc', mixed_terms, right_tiles)
        tile_total = tile_total.reshape(row_count, phys, tile_count * tile_width)
        row_mask = (rows_iota < sector_dims[sector]).astype(jnp.float32)
        return (tile_total * row_mask[:, None, None]).astype(jnp.bfloat16)

    return lax.map(one_sector, jnp.arange(sector_count, dtype=jnp.int32))
```

```python
import jax
import jax.numpy as jnp
from jax import lax
from jax.experimental import pallas as pl
from jax.experimental.pallas import tpu as pltpu
from jax.sharding import PartitionSpec as P


LANE_ROWS = 16
BF16 = jnp.bfloat16
F32 = jnp.float32
VMEM_SPEC = pl.BlockSpec(memory_space=pltpu.VMEM)
SMEM_SPEC = pl.BlockSpec(memory_space=pltpu.SMEM)


def dot(a, b):
    return jnp.dot(a, b, preferred_element_type=F32)


def iota(shape, axis):
    return lax.broadcasted_iota(jnp.int32, shape, axis)


def mix_right(mpo_rows, right_own, right_other, terms, phys, phys_own):
    share, rows, cols = right_own.shape
    right_count = 2 * share
    depth = right_count * LANE_ROWS
    tiles = 2
    groups = terms * phys
    lhs_rows = groups * phys_own * LANE_ROWS
    chunk = LANE_ROWS * phys_own * phys * 2

    def kernel(mpo_ref, own_ref, other_ref, out_ref, lhs):
        core = lax.axis_index("gz")

        @pl.when(pl.program_id(0) == 0)
        def _():
            row = iota((lhs_rows, groups * phys), 0) // LANE_ROWS
            wanted = (row // phys_own) * phys + core * phys_own + row % phys_own
            spread = (iota((lhs_rows, groups * phys), 1) == wanted).astype(F32).astype(BF16)
            tall = dot(spread, mpo_ref[...]).astype(BF16)
            widen = (iota((right_count, depth), 1) // LANE_ROWS == iota((right_count, depth), 0))
            wide = dot(tall, widen.astype(F32).astype(BF16))
            same = iota(wide.shape, 0) % LANE_ROWS == iota(wide.shape, 1) % LANE_ROWS
            lhs[...] = jnp.where(same, wide, 0.0).astype(BF16)

        for t in range(tiles):
            tile = pl.ds(t * LANE_ROWS, LANE_ROWS)
            rhs = jnp.concatenate(
                [
                    own_ref[:, tile, :].reshape(share * LANE_ROWS, cols),
                    other_ref[:, tile, :].reshape(share * LANE_ROWS, cols),
                ],
                0,
            )
            for start in range(0, lhs_rows, chunk):
                part = dot(lhs[start : start + chunk, :], rhs).astype(BF16)
                part = part.reshape(chunk // LANE_ROWS, LANE_ROWS, cols)
                for i in range(chunk // LANE_ROWS):
                    group, p = divmod(start // LANE_ROWS + i, phys_own)
                    out_ref[group, t, :, p * cols : (p + 1) * cols] = part[i]

    row_tiles = rows // LANE_ROWS
    out = pl.pallas_call(
        kernel,
        out_shape=jax.ShapeDtypeStruct((groups, row_tiles, LANE_ROWS, phys_own * cols), BF16),
        grid=(row_tiles // tiles,),
        in_specs=[
            pl.BlockSpec(mpo_rows.shape, lambda t: (0, 0)),
            pl.BlockSpec((share, tiles * LANE_ROWS, cols), lambda t: (0, t, 0)),
            pl.BlockSpec((share, tiles * LANE_ROWS, cols), lambda t: (0, t, 0)),
        ],
        out_specs=pl.BlockSpec(
            (groups, tiles, LANE_ROWS, phys_own * cols), lambda t: (0, t, 0, 0)
        ),
        scratch_shapes=[pltpu.VMEM((lhs_rows, depth), BF16)],
        compiler_params=pltpu.CompilerParams(
            dimension_semantics=("arbitrary",), vmem_limit_bytes=16 << 20
        ),
        cost_estimate=pl.CostEstimate(
            flops=2 * lhs_rows * depth * cols * row_tiles,
            bytes_accessed=2 * groups * rows * phys_own * cols,
            transcendentals=0,
        ),
        name="mix_right",
    )(mpo_rows, right_own, right_other)
    return out.reshape(terms, phys * rows, phys_own * cols)


def apply_block(hop, partner, parts, total, left, mixed, charges, order, dims=None):
    terms = left.shape[0]
    out_cols = mixed.shape[2]
    depth = left.shape[2]
    rows = left.shape[1]
    blocks = [block for block, _ in parts]
    flags = [swapped for _, swapped in parts]
    half, _, cols = blocks[0].shape
    first = total is None

    def kernel(charges_ref, order_ref, *refs):
        refs = list(refs)
        dims_ref = refs.pop(0) if dims is not None else None
        total_ref = refs.pop(0) if not first else None
        left_ref, mixed_ref = refs[0], refs[1]
        block_refs = refs[2 : 2 + len(blocks)]
        out_ref = refs[2 + len(blocks)]
        acc = refs[3 + len(blocks)] if dims is not None else out_ref
        me, core = lax.axis_index("gx"), lax.axis_index("gz")
        shift = order_ref[partner(me, hop)] - order_ref[me] + 1
        acc[...] = jnp.zeros_like(acc) if first else total_ref[...]

        def term(u, carry):
            @pl.when(charges_ref[u] == shift)
            def _():
                env = left_ref[u]
                sums = None
                for ref, swapped in zip(block_refs, flags):
                    which = 1 - core if swapped else core
                    source = jnp.concatenate([ref[q] for q in range(half)], 1)
                    applied = dot(env, source).astype(BF16)
                    begin = pl.multiple_of(which * (half * cols), half * cols)
                    piece = dot(applied, mixed_ref[u, pl.ds(begin, half * cols), :])
                    sums = piece if sums is None else sums + piece
                acc[...] += sums

            return carry

        lax.fori_loop(0, terms, term, 0)
        if dims is not None:
            keep = iota((rows, out_cols), 0) < dims_ref[me]
            masked = jnp.where(keep, acc[...], 0.0).astype(BF16)
            count = out_cols // cols
            for p in range(count):
                out_ref[p] = masked[:, p * cols : (p + 1) * cols]

    scratch = [] if dims is None else [pltpu.VMEM((rows, out_cols), F32)]
    if dims is None:
        out_shape = jax.ShapeDtypeStruct((rows, out_cols), F32)
    else:
        out_shape = jax.ShapeDtypeStruct((out_cols // cols, rows, cols), BF16)
    scalars = [charges, order] + ([] if dims is None else [dims])
    arrays = ([] if first else [total]) + [left, mixed] + blocks
    return pl.pallas_call(
        kernel,
        out_shape=out_shape,
        in_specs=[SMEM_SPEC] * len(scalars) + [VMEM_SPEC] * len(arrays),
        out_specs=VMEM_SPEC,
        scratch_shapes=scratch,
        compiler_params=pltpu.CompilerParams(vmem_limit_bytes=8 << 20),
        cost_estimate=pl.CostEstimate(
            flops=2 * (terms // 3) * rows * half * cols * len(blocks) * (depth + out_cols),
            bytes_accessed=2 * rows * out_cols * 4,
            transcendentals=0,
        ),
        name="apply_block",
    )(*scalars, *arrays)


def gather_blocks(own, axis):
    count = lax.axis_size(axis)
    if count & (count - 1):
        blocks = {
            hop: lax.ppermute(own, axis, [(i, (i + hop) % count) for i in range(count)])
            for hop in range(1, count)
        }
        return blocks, lambda me, hop: lax.rem(me - hop + count, count)
    blocks = {0: own}
    bit = count // 2
    while bit:
        pairs = [(i, i ^ bit) for i in range(count)]
        for hop in list(blocks):
            blocks[hop | bit] = lax.ppermute(blocks[hop], axis, pairs)
        bit //= 2
    del blocks[0]
    return blocks, lambda me, hop: lax.bitwise_xor(me, hop)


def body(state, left_env, mpo_terms, right_env, term_charge, charge_order, sector_dims):
    terms, share, phys, _ = mpo_terms.shape
    cores = lax.axis_size("gz")
    assert state.shape[0] == 1 and cores == 2
    half = phys // cores
    core = lax.axis_index("gz")
    swap = [(0, 1), (1, 0)]
    planes = state[0].transpose(1, 0, 2)
    own = lax.dynamic_slice_in_dim(planes, core * half, half, 0)
    blocks, partner = gather_blocks(own, "gx")
    right_other = lax.ppermute(right_env, "gz", swap)
    mpo_other = lax.ppermute(mpo_terms, "gz", swap)
    mpo_all = jnp.concatenate([mpo_terms, mpo_other], 1)
    mpo_rows = mpo_all.transpose(0, 3, 2, 1).reshape(terms * phys * phys, cores * share)
    mixed = mix_right(mpo_rows, right_env, right_other, terms, phys, half)
    left = left_env[:, 0]

    own_other = lax.dynamic_slice_in_dim(planes, (1 - core) * half, half, 0)
    total = apply_block(
        0, partner, [(own, False), (own_other, True)], None, left, mixed, term_charge, charge_order
    )
    hops = sorted(blocks, key=lambda hop: (bin(hop).count("1"), -hop))
    for hop in hops:
        other = lax.ppermute(blocks[hop], "gz", swap)
        dims = sector_dims if hop == hops[-1] else None
        total = apply_block(
            hop,
            partner,
            [(blocks[hop], False), (other, True)],
            total,
            left,
            mixed,
            term_charge,
            charge_order,
            dims,
        )
    return total.transpose(1, 0, 2)[None]


def solution(mesh):
    return jax.shard_map(
        body,
        mesh=mesh,
        in_specs=(
            P(("ga", "gx"), None, None, "gy"),
            P(None, ("ga", "gx"), None, None),
            P(None, "gz", None, None),
            P("gz", ("ga", "gy"), None),
            P(),
            P("ga"),
            P("ga"),
        ),
        out_specs=P(("ga", "gx"), None, "gz", "gy"),
        check_vma=False,
    )
```

```python
import jax
import jax.numpy as jnp
from jax import lax
from jax.experimental import pallas as pl
from jax.experimental.pallas import tpu as pltpu
from jax.sharding import PartitionSpec as P


LANE_ROWS = 16
BF16 = jnp.bfloat16
F32 = jnp.float32
VMEM_SPEC = pl.BlockSpec(memory_space=pltpu.VMEM)
SMEM_SPEC = pl.BlockSpec(memory_space=pltpu.SMEM)


def dot(a, b):
    return jnp.dot(a, b, preferred_element_type=F32)


def iota(shape, axis):
    return lax.broadcasted_iota(jnp.int32, shape, axis)


def mix_right(mpo_rows, right_own, right_other, terms, phys, phys_own):
    share, rows, cols = right_own.shape
    right_count = 2 * share
    depth = right_count * LANE_ROWS
    tiles = 2
    groups = terms * phys
    lhs_rows = groups * phys_own * LANE_ROWS
    chunk = LANE_ROWS * phys_own * phys * 2

    def kernel(mpo_ref, own_ref, other_ref, out_ref, lhs):
        core = lax.axis_index("gz")

        @pl.when(pl.program_id(0) == 0)
        def _():
            row = iota((lhs_rows, groups * phys), 0) // LANE_ROWS
            wanted = (row // phys_own) * phys + core * phys_own + row % phys_own
            spread = (iota((lhs_rows, groups * phys), 1) == wanted).astype(F32).astype(BF16)
            tall = dot(spread, mpo_ref[...]).astype(BF16)
            widen = (iota((right_count, depth), 1) // LANE_ROWS == iota((right_count, depth), 0))
            wide = dot(tall, widen.astype(F32).astype(BF16))
            same = iota(wide.shape, 0) % LANE_ROWS == iota(wide.shape, 1) % LANE_ROWS
            lhs[...] = jnp.where(same, wide, 0.0).astype(BF16)

        for t in range(tiles):
            tile = pl.ds(t * LANE_ROWS, LANE_ROWS)
            rhs = jnp.concatenate(
                [
                    own_ref[:, tile, :].reshape(share * LANE_ROWS, cols),
                    other_ref[:, tile, :].reshape(share * LANE_ROWS, cols),
                ],
                0,
            )
            for start in range(0, lhs_rows, chunk):
                part = dot(lhs[start : start + chunk, :], rhs).astype(BF16)
                part = part.reshape(chunk // LANE_ROWS, LANE_ROWS, cols)
                for i in range(chunk // LANE_ROWS):
                    group, p = divmod(start // LANE_ROWS + i, phys_own)
                    out_ref[group, t, :, p * cols : (p + 1) * cols] = part[i]

    row_tiles = rows // LANE_ROWS
    out = pl.pallas_call(
        kernel,
        out_shape=jax.ShapeDtypeStruct((groups, row_tiles, LANE_ROWS, phys_own * cols), BF16),
        grid=(row_tiles // tiles,),
        in_specs=[
            pl.BlockSpec(mpo_rows.shape, lambda t: (0, 0)),
            pl.BlockSpec((share, tiles * LANE_ROWS, cols), lambda t: (0, t, 0)),
            pl.BlockSpec((share, tiles * LANE_ROWS, cols), lambda t: (0, t, 0)),
        ],
        out_specs=pl.BlockSpec(
            (groups, tiles, LANE_ROWS, phys_own * cols), lambda t: (0, t, 0, 0)
        ),
        scratch_shapes=[pltpu.VMEM((lhs_rows, depth), BF16)],
        compiler_params=pltpu.CompilerParams(
            dimension_semantics=("arbitrary",), vmem_limit_bytes=16 << 20
        ),
        cost_estimate=pl.CostEstimate(
            flops=2 * lhs_rows * depth * cols * row_tiles,
            bytes_accessed=2 * groups * rows * phys_own * cols,
            transcendentals=0,
        ),
        name="mix_right",
    )(mpo_rows, right_own, right_other)
    return out.reshape(terms, phys * rows, phys_own * cols)


def apply_block(hop, partner, parts, total, left, mixed, charges, order, dims=None):
    terms = left.shape[0]
    out_cols = mixed.shape[2]
    depth = left.shape[2]
    rows = left.shape[1]
    blocks = [block for block, _ in parts]
    flags = [swapped for _, swapped in parts]
    half, _, cols = blocks[0].shape
    first = total is None

    def kernel(charges_ref, order_ref, *refs):
        refs = list(refs)
        dims_ref = refs.pop(0) if dims is not None else None
        total_ref = refs.pop(0) if not first else None
        left_ref, mixed_ref = refs[0], refs[1]
        block_refs = refs[2 : 2 + len(blocks)]
        out_ref = refs[2 + len(blocks)]
        acc = refs[3 + len(blocks)] if dims is not None else out_ref
        me, core = lax.axis_index("gx"), lax.axis_index("gz")
        shift = order_ref[partner(me, hop)] - order_ref[me] + 1
        acc[...] = jnp.zeros_like(acc) if first else total_ref[...]

        def term(u, carry):
            @pl.when(charges_ref[u] == shift)
            def _():
                env = left_ref[u]
                sums = None
                for ref, swapped in zip(block_refs, flags):
                    which = 1 - core if swapped else core
                    source = jnp.concatenate([ref[q] for q in range(half)], 1)
                    applied = dot(env, source).astype(BF16)
                    begin = pl.multiple_of(which * (half * cols), half * cols)
                    piece = dot(applied, mixed_ref[u, pl.ds(begin, half * cols), :])
                    sums = piece if sums is None else sums + piece
                acc[...] += sums

            return carry

        lax.fori_loop(0, terms, term, 0)
        if dims is not None:
            keep = iota((rows, out_cols), 0) < dims_ref[me]
            masked = jnp.where(keep, acc[...], 0.0).astype(BF16)
            count = out_cols // cols
            for p in range(count):
                out_ref[p] = masked[:, p * cols : (p + 1) * cols]

    scratch = [] if dims is None else [pltpu.VMEM((rows, out_cols), F32)]
    if dims is None:
        out_shape = jax.ShapeDtypeStruct((rows, out_cols), F32)
    else:
        out_shape = jax.ShapeDtypeStruct((out_cols // cols, rows, cols), BF16)
    scalars = [charges, order] + ([] if dims is None else [dims])
    arrays = ([] if first else [total]) + [left, mixed] + blocks
    return pl.pallas_call(
        kernel,
        out_shape=out_shape,
        in_specs=[SMEM_SPEC] * len(scalars) + [VMEM_SPEC] * len(arrays),
        out_specs=VMEM_SPEC,
        scratch_shapes=scratch,
        compiler_params=pltpu.CompilerParams(vmem_limit_bytes=8 << 20),
        cost_estimate=pl.CostEstimate(
            flops=2 * (terms // 3) * rows * half * cols * len(blocks) * (depth + out_cols),
            bytes_accessed=2 * rows * out_cols * 4,
            transcendentals=0,
        ),
        name="apply_block",
    )(*scalars, *arrays)


def gather_blocks(own, axis):
    count = lax.axis_size(axis)
    if count & (count - 1):
        blocks = {}
        for hop in range(1, count):
            pairs = [(i, (i + hop) % count) for i in range(count)]
            blocks[hop] = lax.ppermute(own, axis, pairs)
        return blocks, lambda me, hop: lax.rem(me - hop + count, count)
    blocks = {0: own}
    bit = count // 2
    while bit:
        pairs = [(i, i ^ bit) for i in range(count)]
        for hop in list(blocks):
            blocks[hop | bit] = lax.ppermute(blocks[hop], axis, pairs)
        bit //= 2
    del blocks[0]
    return blocks, lambda me, hop: lax.bitwise_xor(me, hop)


def use_order(count):
    return sorted(range(1, count), key=lambda hop: (bin(hop).count("1"), -hop))


def step(state, left_env, mpo_terms, right_env, term_charge, charge_order, sector_dims):
    terms, share, phys, _ = mpo_terms.shape
    cores = lax.axis_size("gz")
    assert state.shape[0] == 1 and cores == 2
    half = phys // cores
    core = lax.axis_index("gz")
    swap = [(0, 1), (1, 0)]
    planes = state[0].transpose(1, 0, 2)
    own = lax.dynamic_slice_in_dim(planes, core * half, half, 0)
    blocks, partner = gather_blocks(own, "gx")
    right_other = lax.ppermute(right_env, "gz", swap)
    mpo_other = lax.ppermute(mpo_terms, "gz", swap)
    mpo_all = jnp.concatenate([mpo_terms, mpo_other], 1)
    mpo_rows = mpo_all.transpose(0, 3, 2, 1).reshape(terms * phys * phys, cores * share)
    mixed = mix_right(mpo_rows, right_env, right_other, terms, phys, half)
    left = left_env[:, 0]

    own_other = lax.dynamic_slice_in_dim(planes, (1 - core) * half, half, 0)
    own_parts = [(own, False), (own_other, True)]
    total = apply_block(
        0, partner, own_parts, None, left, mixed, term_charge, charge_order
    )
    hops = use_order(lax.axis_size("gx"))
    for hop in hops:
        other = lax.ppermute(blocks[hop], "gz", swap)
        dims = sector_dims if hop == hops[-1] else None
        parts = [(blocks[hop], False), (other, True)]
        total = apply_block(
            hop, partner, parts, total, left, mixed, term_charge, charge_order, dims
        )
    return total.transpose(1, 0, 2)[None]


def solution(mesh):
    return jax.shard_map(
        step,
        mesh=mesh,
        in_specs=(
            P(("ga", "gx"), None, None, "gy"),
            P(None, ("ga", "gx"), None, None),
            P(None, "gz", None, None),
            P("gz", ("ga", "gy"), None),
            P(),
            P("ga"),
            P("ga"),
        ),
        out_specs=P(("ga", "gx"), None, "gz", "gy"),
        check_vma=False,
    )
```

```python
import jax
import jax.numpy as jnp
from jax import lax
from jax.experimental import pallas as pl
from jax.experimental.pallas import tpu as pltpu
from jax.sharding import PartitionSpec as P


LANE_ROWS = 16
MIX_ROWS = 512
MIX_TILES = 8
BF16 = jnp.bfloat16
F32 = jnp.float32
VMEM_SPEC = pl.BlockSpec(memory_space=pltpu.VMEM)
SMEM_SPEC = pl.BlockSpec(memory_space=pltpu.SMEM)


def dot(a, b):
    return jnp.dot(a, b, preferred_element_type=F32)


def iota(shape, axis):
    return lax.broadcasted_iota(jnp.int32, shape, axis)


def mix_right(mpo_rows, right_own, right_other, terms, phys, phys_own):
    share, rows, cols = right_own.shape
    right_count = 2 * share
    depth = right_count * LANE_ROWS
    groups = terms * phys
    lhs_rows = groups * phys_own * LANE_ROWS
    width = MIX_TILES * LANE_ROWS
    steps = rows // width
    chunk = min(lhs_rows, MIX_ROWS)

    def kernel(mpo_ref, own_hbm, other_hbm, out_ref, lhs, own_ref, other_ref, sems):
        core = lax.axis_index("gz")
        copies = [
            pltpu.make_async_copy(source, target, sems.at[i])
            for i, (source, target) in enumerate([(own_hbm, own_ref), (other_hbm, other_ref)])
        ]
        for copy in copies:
            copy.start()
        shape = (groups * phys_own, groups * phys)
        row = iota(shape, 0)
        wanted = (row // phys_own) * phys + core * phys_own + row % phys_own
        pick = (iota(shape, 1) == wanted).astype(F32).astype(BF16)
        picked = dot(pick, mpo_ref[...]).astype(BF16)
        widen = iota((right_count, depth), 1) // LANE_ROWS == iota((right_count, depth), 0)
        wide = dot(picked, widen.astype(F32).astype(BF16))
        shape = (LANE_ROWS, depth)
        same = (iota(shape, 0) == iota(shape, 1) % LANE_ROWS).astype(F32)
        tall = wide[:, None, :] * same[None, :, :]
        lhs[...] = tall.reshape(lhs_rows, depth).astype(BF16)
        for copy in copies:
            copy.wait()

        def tile(step, carry):
            parts = []
            for t in range(MIX_TILES):
                begin = pl.multiple_of(step * width + t * LANE_ROWS, LANE_ROWS)
                here = pl.ds(begin, LANE_ROWS)
                sides = [ref[:, here, :].reshape(-1, cols) for ref in (own_ref, other_ref)]
                parts.append(jnp.concatenate(sides, 0))
            rhs = jnp.concatenate(parts, 1)
            for start in range(0, lhs_rows, chunk):
                part = dot(lhs[start : start + chunk, :], rhs).astype(BF16)
                part = part.reshape(chunk // LANE_ROWS, LANE_ROWS, MIX_TILES * cols)
                for i in range(chunk // LANE_ROWS):
                    group, p = divmod(start // LANE_ROWS + i, phys_own)
                    for t in range(MIX_TILES):
                        out_ref[group, step * MIX_TILES + t, :, p * cols : (p + 1) * cols] = part[
                            i, :, t * cols : (t + 1) * cols
                        ]
            return carry

        lax.fori_loop(0, steps, tile, 0)

    row_tiles = rows // LANE_ROWS
    out = pl.pallas_call(
        kernel,
        out_shape=jax.ShapeDtypeStruct((groups, row_tiles, LANE_ROWS, phys_own * cols), BF16),
        in_specs=[VMEM_SPEC, pl.BlockSpec(memory_space=pl.ANY), pl.BlockSpec(memory_space=pl.ANY)],
        out_specs=VMEM_SPEC,
        scratch_shapes=[
            pltpu.VMEM((lhs_rows, depth), BF16),
            pltpu.VMEM(right_own.shape, BF16),
            pltpu.VMEM(right_own.shape, BF16),
            pltpu.SemaphoreType.DMA((2,)),
        ],
        compiler_params=pltpu.CompilerParams(vmem_limit_bytes=20 << 20),
        cost_estimate=pl.CostEstimate(
            flops=2 * lhs_rows * depth * cols * row_tiles,
            bytes_accessed=2 * groups * rows * phys_own * cols,
            transcendentals=0,
        ),
        name="mix_right",
    )(mpo_rows, right_own, right_other)
    return out.reshape(terms, phys * rows, phys_own * cols)


def apply_blocks(hops, partner, blocks, total, left, mixed, charges, order, dims=None):
    terms, rows, depth = left.shape
    out_cols = mixed.shape[2]
    half, _, cols = blocks[0].shape
    first, last = total is None, dims is not None

    def kernel(charges_ref, order_ref, *refs):
        refs = list(refs)
        dims_ref = refs.pop(0) if last else None
        total_ref = None if first else refs.pop(0)
        left_ref, mixed_ref = refs[:2]
        block_refs = refs[2 : 2 + len(blocks)]
        out_ref, term_list, block_list, sources = refs[2 + len(blocks) :][:4]
        acc = refs[-1] if last else out_ref
        me, core = lax.axis_index("gx"), lax.axis_index("gz")
        count = jnp.int32(0)
        for i, hop in enumerate(hops):
            shift = order_ref[partner(me, hop)] - order_ref[me] + 1
            for u in range(terms):
                term_list[count] = u
                block_list[count] = i
                count += (charges_ref[u] == shift).astype(jnp.int32)
            for q in range(half):
                sources[i, core * half + q] = block_refs[2 * i][q]
                sources[i, (1 - core) * half + q] = block_refs[2 * i + 1][q]
        acc[...] = jnp.zeros_like(acc) if first else total_ref[...]

        def add(start, many):
            sums = None
            for k in range(many):
                u, i = term_list[start + k], block_list[start + k]
                env = left_ref[u]
                applied = [dot(env, sources[i, q]).astype(BF16) for q in range(2 * half)]
                piece = dot(jnp.concatenate(applied, 1), mixed_ref[u])
                sums = piece if sums is None else sums + piece
            acc[...] += sums

        def four(i, carry):
            add(4 * i, 4)
            return carry

        lax.fori_loop(0, count // 4, four, 0)
        rest = count % 4

        @pl.when(rest >= 2)
        def _():
            add(count - rest, 2)

        @pl.when(rest % 2 == 1)
        def _():
            add(count - 1, 1)

        if last:
            keep = iota((rows, out_cols), 0) < dims_ref[me]
            masked = jnp.where(keep, acc[...], 0.0)
            out_ref[...] = masked.reshape(rows, out_cols // cols, cols).astype(BF16)

    slots = terms * len(hops) + 1
    scratch = [
        pltpu.SMEM((slots,), jnp.int32),
        pltpu.SMEM((slots,), jnp.int32),
        pltpu.VMEM((len(hops), 2 * half, depth, cols), BF16),
    ]
    if last:
        scratch.append(pltpu.VMEM((rows, out_cols), F32))
        out_shape = jax.ShapeDtypeStruct((rows, out_cols // cols, cols), BF16)
    else:
        out_shape = jax.ShapeDtypeStruct((rows, out_cols), F32)
    scalars = [charges, order] + ([dims] if last else [])
    arrays = ([] if first else [total]) + [left, mixed] + list(blocks)
    block_bytes = 2 * depth * half * 2 * cols
    return pl.pallas_call(
        kernel,
        out_shape=out_shape,
        in_specs=[SMEM_SPEC] * len(scalars) + [VMEM_SPEC] * len(arrays),
        out_specs=VMEM_SPEC,
        scratch_shapes=scratch,
        compiler_params=pltpu.CompilerParams(
            vmem_limit_bytes=(8 << 20) + 2 * len(hops) * block_bytes
        ),
        cost_estimate=pl.CostEstimate(
            flops=2 * (terms // 3) * rows * 2 * half * cols * len(hops) * (depth + out_cols),
            bytes_accessed=2 * rows * out_cols * 4,
            transcendentals=0,
        ),
        name="apply_blocks",
    )(*scalars, *arrays)


def gather_blocks(own, axis):
    count = lax.axis_size(axis)
    if count & (count - 1):
        blocks = {}
        for hop in range(1, count):
            pairs = [(i, (i + hop) % count) for i in range(count)]
            blocks[hop] = lax.ppermute(own, axis, pairs)
        return blocks, lambda me, hop: lax.rem(me - hop + count, count)
    blocks = {0: own}
    bit = count // 2
    while bit:
        pairs = [(i, i ^ bit) for i in range(count)]
        for hop in list(blocks):
            blocks[hop | bit] = lax.ppermute(blocks[hop], axis, pairs)
        bit //= 2
    del blocks[0]
    return blocks, lambda me, hop: lax.bitwise_xor(me, hop)


def use_stages(count):
    order = sorted(range(1, count), key=lambda hop: (bin(hop).count("1"), -hop))
    return [hops for hops in ([0] + order[:-1], order[-1:]) if hops]


def step(state, left_env, mpo_terms, right_env, term_charge, charge_order, sector_dims):
    terms, share, phys, _ = mpo_terms.shape
    cores = lax.axis_size("gz")
    assert state.shape[0] == 1 and cores == 2
    half = phys // cores
    core = lax.axis_index("gz")
    swap = [(0, 1), (1, 0)]
    planes = state[0].transpose(1, 0, 2)
    own = lax.dynamic_slice_in_dim(planes, core * half, half, 0)
    blocks, partner = gather_blocks(own, "gx")
    right_other = lax.ppermute(right_env, "gz", swap)
    mpo_other = lax.ppermute(mpo_terms, "gz", swap)
    mpo_all = jnp.concatenate([mpo_terms, mpo_other], 1)
    mpo_rows = mpo_all.transpose(0, 3, 2, 1).reshape(terms * phys * phys, cores * share)
    mixed = mix_right(mpo_rows, right_env, right_other, terms, phys, half)
    left = left_env[:, 0]

    own_other = lax.dynamic_slice_in_dim(planes, (1 - core) * half, half, 0)
    pairs = {0: (own, own_other)}
    for hop, block in blocks.items():
        pairs[hop] = (block, lax.ppermute(block, "gz", swap))
    total = None
    stages = use_stages(lax.axis_size("gx"))
    for number, hops in enumerate(stages):
        dims = sector_dims if number == len(stages) - 1 else None
        parts = [part for hop in hops for part in pairs[hop]]
        total = apply_blocks(
            hops, partner, parts, total, left, mixed, term_charge, charge_order, dims
        )
    return total[None]


def solution(mesh):
    return jax.shard_map(
        step,
        mesh=mesh,
        in_specs=(
            P(("ga", "gx"), None, None, "gy"),
            P(None, ("ga", "gx"), None, None),
            P(None, "gz", None, None),
            P("gz", ("ga", "gy"), None),
            P(),
            P("ga"),
            P("ga"),
        ),
        out_specs=P(("ga", "gx"), None, "gz", "gy"),
        check_vma=False,
    )
```

```python
import jax
import jax.numpy as jnp
from jax import lax
from jax.experimental import pallas as pl
from jax.experimental.pallas import tpu as pltpu
from jax.sharding import PartitionSpec as P


LANE_ROWS = 16
MIX_ROWS = 512
MIX_TILES = 8
BF16 = jnp.bfloat16
F32 = jnp.float32
VMEM_SPEC = pl.BlockSpec(memory_space=pltpu.VMEM)
SMEM_SPEC = pl.BlockSpec(memory_space=pltpu.SMEM)


def dot(a, b):
    return jnp.dot(a, b, preferred_element_type=F32)


def iota(shape, axis):
    return lax.broadcasted_iota(jnp.int32, shape, axis)


def spread_mpo(mpo_own, mpo_other, share, phys, phys_own):
    terms = mpo_own.shape[1]
    rows = terms * phys * phys_own
    depth = 2 * share * LANE_ROWS
    pairs = phys * phys

    def kernel(own_ref, other_ref, out_ref):
        core = lax.axis_index("gz")
        shape = (rows, terms)
        spread = iota(shape, 0) // (phys * phys_own) == iota(shape, 1)
        spread = spread.astype(F32).astype(BF16)
        shape = (rows, share * pairs)
        row, column = iota(shape, 0), iota(shape, 1) % pairs
        wanted = (core * phys_own + row % phys_own) * phys + row // phys_own % phys
        wide = None
        for side, ref in enumerate((own_ref, other_ref)):
            chosen = lax.dot_general(
                spread, ref[...], (((1,), (1,)), ((), ())), preferred_element_type=F32
            )
            chosen = jnp.where(column == wanted, chosen, 0.0).astype(BF16)
            shape = (share * pairs, depth)
            widen = iota(shape, 0) // pairs + side * share == iota(shape, 1) // LANE_ROWS
            part = dot(chosen, widen.astype(F32).astype(BF16))
            wide = part if wide is None else wide + part
        shape = (LANE_ROWS, depth)
        same = (iota(shape, 0) == iota(shape, 1) % LANE_ROWS).astype(F32)
        tall = wide[:, None, :] * same[None, :, :]
        out_ref[...] = tall.reshape(rows * LANE_ROWS, depth).astype(BF16)

    return pl.pallas_call(
        kernel,
        out_shape=jax.ShapeDtypeStruct((rows * LANE_ROWS, depth), BF16),
        in_specs=[VMEM_SPEC] * 2,
        out_specs=VMEM_SPEC,
        compiler_params=pltpu.CompilerParams(vmem_limit_bytes=8 << 20),
        cost_estimate=pl.CostEstimate(
            flops=1 << 28, bytes_accessed=2 * rows * LANE_ROWS * depth, transcendentals=0
        ),
        name="spread_mpo",
    )(mpo_own, mpo_other)


def mix_right(lhs, right_own, right_other, terms, phys, phys_own):
    rows, cols = right_own.shape[1:]
    lhs_rows, depth = lhs.shape
    groups = terms * phys
    width = MIX_TILES * LANE_ROWS
    chunk = min(lhs_rows, MIX_ROWS)
    row_tiles = rows // LANE_ROWS

    def kernel(lhs_ref, own_ref, other_ref, out_ref):
        def tile(step, carry):
            parts = []
            for t in range(MIX_TILES):
                begin = pl.multiple_of(step * width + t * LANE_ROWS, LANE_ROWS)
                here = pl.ds(begin, LANE_ROWS)
                sides = [ref[:, here, :].reshape(-1, cols) for ref in (own_ref, other_ref)]
                parts.append(jnp.concatenate(sides, 0))
            rhs = jnp.concatenate(parts, 1)
            for start in range(0, lhs_rows, chunk):
                part = dot(lhs_ref[start : start + chunk, :], rhs).astype(BF16)
                part = part.reshape(chunk // LANE_ROWS, LANE_ROWS, MIX_TILES * cols)
                for i in range(chunk // LANE_ROWS):
                    group, p = divmod(start // LANE_ROWS + i, phys_own)
                    for t in range(MIX_TILES):
                        out_ref[group, step * MIX_TILES + t, :, p * cols : (p + 1) * cols] = part[
                            i, :, t * cols : (t + 1) * cols
                        ]
            return carry

        lax.fori_loop(0, rows // width, tile, 0)

    out = pl.pallas_call(
        kernel,
        out_shape=jax.ShapeDtypeStruct((groups, row_tiles, LANE_ROWS, phys_own * cols), BF16),
        in_specs=[VMEM_SPEC] * 3,
        out_specs=VMEM_SPEC,
        compiler_params=pltpu.CompilerParams(vmem_limit_bytes=20 << 20),
        cost_estimate=pl.CostEstimate(
            flops=2 * lhs_rows * depth * cols * row_tiles,
            bytes_accessed=2 * groups * rows * phys_own * cols,
            transcendentals=0,
        ),
        name="mix_right",
    )(lhs, right_own, right_other)
    return out.reshape(terms, phys * rows, phys_own * cols)


def apply_blocks(
    hops, sides, partner, blocks, total, left, mixed, charges, order, dims=None
):
    terms, rows, depth = left.shape
    out_cols = mixed.shape[2]
    half, _, cols = blocks[0][0].shape
    held = half * len(sides)
    first, last = total is None, dims is not None

    def kernel(charges_ref, order_ref, *refs):
        refs = list(refs)
        dims_ref = refs.pop(0) if last else None
        total_ref = None if first else refs.pop(0)
        left_ref, mixed_ref = refs[:2]
        block_refs = refs[2 : 2 + len(hops) * len(sides)]
        out_ref, term_list, block_list, sources = refs[2 + len(block_refs) :][:4]
        acc = refs[-1] if last else out_ref
        me, core = lax.axis_index("gx"), lax.axis_index("gz")
        whole = len(sides) == 2
        begin = 0 if whole else (1 - core if sides[0] else core) * half * cols
        begin = begin if whole else pl.multiple_of(begin, half * cols)
        count = jnp.int32(0)
        for i, hop in enumerate(hops):
            shift = order_ref[partner(me, hop)] - order_ref[me] + 1
            for u in range(terms):
                term_list[count] = u
                block_list[count] = i
                count += (charges_ref[u] == shift).astype(jnp.int32)
            for k, side in enumerate(sides):
                which = (1 - core if side else core) if whole else 0
                for q in range(half):
                    sources[i, which * half + q] = block_refs[i * len(sides) + k][q]
        acc[...] = jnp.zeros_like(acc) if first else total_ref[...]

        def add(start, many):
            sums = None
            for k in range(many):
                u, i = term_list[start + k], block_list[start + k]
                env = left_ref[u]
                applied = [dot(env, sources[i, q]).astype(BF16) for q in range(held)]
                weights = mixed_ref[u, pl.ds(begin, held * cols), :]
                piece = dot(jnp.concatenate(applied, 1), weights)
                sums = piece if sums is None else sums + piece
            acc[...] += sums

        def four(i, carry):
            add(4 * i, 4)
            return carry

        lax.fori_loop(0, count // 4, four, 0)
        rest = count % 4

        @pl.when(rest >= 2)
        def _():
            add(count - rest, 2)

        @pl.when(rest % 2 == 1)
        def _():
            add(count - 1, 1)

        if last:
            keep = iota((rows, out_cols), 0) < dims_ref[me]
            masked = jnp.where(keep, acc[...], 0.0)
            out_ref[...] = masked.reshape(rows, out_cols // cols, cols).astype(BF16)

    slots = terms * len(hops) + 1
    scratch = [
        pltpu.SMEM((slots,), jnp.int32),
        pltpu.SMEM((slots,), jnp.int32),
        pltpu.VMEM((len(hops), held, depth, cols), BF16),
    ]
    if last:
        scratch.append(pltpu.VMEM((rows, out_cols), F32))
        out_shape = jax.ShapeDtypeStruct((rows, out_cols // cols, cols), BF16)
    else:
        out_shape = jax.ShapeDtypeStruct((rows, out_cols), F32)
    scalars = [charges, order] + ([dims] if last else [])
    arrays = ([] if first else [total]) + [left, mixed]
    arrays += [block for parts in blocks for block in parts]
    block_bytes = 2 * depth * held * cols
    return pl.pallas_call(
        kernel,
        out_shape=out_shape,
        in_specs=[SMEM_SPEC] * len(scalars) + [VMEM_SPEC] * len(arrays),
        out_specs=VMEM_SPEC,
        scratch_shapes=scratch,
        compiler_params=pltpu.CompilerParams(
            vmem_limit_bytes=(8 << 20) + 2 * len(hops) * block_bytes
        ),
        cost_estimate=pl.CostEstimate(
            flops=2 * (terms // 3) * rows * held * cols * len(hops) * (depth + out_cols),
            bytes_accessed=2 * rows * out_cols * 4,
            transcendentals=0,
        ),
        name="apply_blocks",
    )(*scalars, *arrays)


def gather_blocks(own, axis):
    count = lax.axis_size(axis)
    blocks = {0: own}
    if count & (count - 1):
        steps = [(0, hop, [(i, (i + hop) % count) for i in range(count)]) for hop in range(1, count)]
        partner = lambda me, hop: lax.rem(me - hop + count, count)
    else:
        steps = []
        bit = count // 2
        while bit:
            pairs = [(i, i ^ bit) for i in range(count)]
            held = [0] + [hop for _, hop, _ in steps]
            steps += [(hop, hop | bit, pairs) for hop in held]
            bit //= 2
        partner = lambda me, hop: lax.bitwise_xor(me, hop)
    for source, hop, pairs in steps:
        blocks[hop] = lax.ppermute(blocks[source], axis, pairs)
    return blocks, partner


def use_stages(count):
    order = sorted(range(1, count), key=lambda hop: (bin(hop).count("1"), -hop))
    stages = [([0], (0, 1)), (order[:-1], (0, 1)), (order[-1:], (0,)), (order[-1:], (1,))]
    return [stage for stage in stages if stage[0]]


def step(state, left_env, mpo_terms, right_env, term_charge, charge_order, sector_dims):
    terms, share, phys, _ = mpo_terms.shape
    cores = lax.axis_size("gz")
    assert state.shape[0] == 1 and cores == 2
    half = phys // cores
    core = lax.axis_index("gz")
    swap = [(0, 1), (1, 0)]
    planes = state[0].transpose(1, 0, 2)
    own = lax.dynamic_slice_in_dim(planes, core * half, half, 0)
    own_other = lax.dynamic_slice_in_dim(planes, (1 - core) * half, half, 0)
    own, own_other, right_sent = lax.optimization_barrier((own, own_other, right_env))
    blocks, partner = gather_blocks(own, "gx")
    right_other = lax.ppermute(right_sent, "gz", swap)
    mpo_rows = mpo_terms.transpose(1, 2, 3, 0).reshape(share * phys * phys, terms)
    mpo_other = lax.ppermute(mpo_rows, "gz", swap)
    lhs = spread_mpo(mpo_rows, mpo_other, share, phys, half)
    mixed = mix_right(lhs, right_env, right_other, terms, phys, half)
    left = left_env[:, 0]

    halves = {0: (own, own_other)}
    for hop, block in blocks.items():
        if hop:
            halves[hop] = (block, lax.ppermute(block, "gz", swap))
    total = None
    stages = use_stages(lax.axis_size("gx"))
    for number, (hops, sides) in enumerate(stages):
        dims = sector_dims if number == len(stages) - 1 else None
        parts = [[halves[hop][side] for side in sides] for hop in hops]
        total = apply_blocks(
            hops, sides, partner, parts, total, left, mixed, term_charge, charge_order, dims
        )
    return total[None]


def solution(mesh):
    return jax.shard_map(
        step,
        mesh=mesh,
        in_specs=(
            P(("ga", "gx"), None, None, "gy"),
            P(None, ("ga", "gx"), None, None),
            P(None, "gz", None, None),
            P("gz", ("ga", "gy"), None),
            P(),
            P("ga"),
            P("ga"),
        ),
        out_specs=P(("ga", "gx"), None, "gz", "gy"),
        check_vma=False,
    )
```
